32 devices in a mesh: leaf: 4 (over z), rows: 8 (over y, x, core).
Axes of the slice: x: 2, y: 2, z: 4, core: 2. Of those that a mesh axis runs over, the one named last changes fastest.
Arguments:
- rhs: float32 [131072, 256], P(('leaf', 'rows')), may hold values from -6 to 6
- u_basis: float32 [4, 131072, 128], P(None, ('leaf', 'rows')), may hold values from -0.5 to 0.5
- v_basis: float32 [4, 131072, 128], P(None, ('leaf', 'rows')), may hold values from -0.06629126 to 0.06629126
- cap_inv: float32 [15, 256, 256], replicated, may hold values from -0.1125 to 1.1125
Outputs:
- solved: float32 [131072, 256], P(('leaf', 'rows'))
The draws below stay inside these ranges and needn't reach their ends.
All inputs are finite; a program needn't handle non-finite values.
Results may differ from the reference program's by a relative error of at most 0.00012.
Values sent between devices are 32-bit elements; how exact they have to be, the bound alone decides.
A program may use at most 128 MiB of HBM per device.

```python
import jax
import jax.numpy as jnp
from jax import lax

RANK = 128
NRHS = 256
LEVELS = 4
NODES = 15
TOTAL_ROWS = 131072


def draw_v_basis(key, part):
    level = jnp.arange(LEVELS, dtype=jnp.float32)[:, None, None]
    scale = jnp.sqrt(2.0 ** (level + 1.0) / TOTAL_ROWS)
    base = jnp.clip(jax.random.normal(key, (LEVELS, TOTAL_ROWS, RANK), jnp.float32), -6.0, 6.0)
    return base * scale


def draw_cap_inv(key, part):
    order = 2 * RANK
    base = jnp.clip(jax.random.normal(key, (NODES, order, order), jnp.float32), -3.0, 3.0)
    spread = 0.6 / order ** 0.5
    return jnp.eye(order, dtype=jnp.float32)[None] + base * spread


def levels(own_key, dims, split, smallest, top_value):
    gain, own = 1.0, jax.random.fold_in(own_key, 6)
    for axis_at, parts in split:
        steps = jnp.exp(jax.random.uniform(jax.random.fold_in(own, axis_at), (parts,), jnp.float32, smallest / len(split), top_value / len(split)))
        gain = gain * jnp.repeat(steps, dims[axis_at] // parts).reshape([-1 if axis == axis_at else 1 for axis in range(len(dims))])
    return gain


def noise(rng, dims, deviation, bound, split=(), kind=jnp.bfloat16):
    level = levels(rng, dims, split, -0.22, 0.18) if split else 1.0
    values = jax.random.normal(rng, dims, jnp.float32) * deviation * level
    return jnp.minimum(jnp.maximum(values, -bound), bound).astype(kind)


def setup_inputs(seed: int = 0) -> dict:
    keys = jax.random.split(jax.random.key(seed), 5)
    rhs = noise(keys[0], (TOTAL_ROWS, NRHS), 1.0, 6.0, ((0, 32),), jnp.float32)
    u_basis = noise(keys[1], (LEVELS, TOTAL_ROWS, RANK), RANK ** -0.5, 0.5, ((1, 32),), jnp.float32)
    v_basis = draw_v_basis(jax.random.fold_in(keys[4], 71), 0)
    cap_inv = draw_cap_inv(jax.random.fold_in(keys[4], 71), 0)
    return {"rhs": rhs, "u_basis": u_basis, "v_basis": v_basis, "cap_inv": cap_inv}


def reference(rhs, u_basis, v_basis, cap_inv):
    highest = lax.Precision.HIGHEST
    field = rhs
    for level in range(LEVELS):
        kids = 2 ** (level + 1)
        span = TOTAL_ROWS // kids
        shaped = field.reshape(kids, span, NRHS)
        v_rows = v_basis[level].reshape(kids, span, RANK)
        proj = jnp.einsum('csk,csr->ckr', v_rows, shaped, precision=highest)
        stacked = proj.reshape(kids // 2, 2 * RANK, NRHS)
        start = 2 ** level - 1
        caps = cap_inv[start:start + kids // 2]
        coef = jnp.einsum('nij,njr->nir', caps, stacked, precision=highest).reshape(kids, RANK, NRHS)
        u_rows = u_basis[level].reshape(kids, span, RANK)
        field = field - jnp.einsum('csk,ckr->csr', u_rows, coef, precision=highest).reshape(TOTAL_ROWS, NRHS)
    return field
```

```python
import jax
import jax.numpy as jnp
from jax import lax
from jax.experimental import pallas as pl
from jax.experimental.pallas import tpu as pltpu
from jax.sharding import PartitionSpec as P

MESH = pl.DeviceIdType.MESH
CHUNK = 512
F32 = jnp.float32
BF16 = jnp.bfloat16


def split(x):
    high = x.astype(BF16)
    return high, (x - high.astype(F32)).astype(BF16)


def dot(a, b):
    return jnp.dot(a, b, preferred_element_type=F32)


def dot_rows(a, b):
    return lax.dot_general(a, b, (((0,), (0,)), ((), ())), preferred_element_type=F32)


def dot3(a, b):
    ah, al = split(a)
    bh, bl = split(b)
    return dot(ah, bh) + dot(al, bh) + dot(ah, bl)


def make_kernel(levels, rows, rank, width, leaves, lines):
    bits = (leaves * lines).bit_length() - 1
    line_bits = lines.bit_length() - 1
    half = rank // 2
    steps = rows // CHUNK
    tops = [bits - level - 1 for level in range(levels)]
    first = [sum(top + 1 for top in tops[:level]) for level in range(levels)]
    exchanges = sum(top + 1 for top in tops)
    widths = [width + level * rank for level in range(levels)]

    def kernel(rhs_hbm, u_hbm, v_hbm, cap_hbm, out_hbm, *scratch):
        rhs, u, v, cap, high, low, coef = scratch[:7]
        acc = scratch[7 : 7 + levels]
        cur = scratch[7 + levels : 7 + 2 * levels]
        recv = scratch[7 + 2 * levels : 7 + 3 * levels]
        stk = scratch[7 + 3 * levels : 7 + 4 * levels]
        rhs_sem, v0_sem, u_sem, v_sem, cap_sem, out_sem, tx, rx = scratch[7 + 4 * levels :]

        leaf = lax.axis_index("leaf")
        line = lax.axis_index("rows")
        flat = leaf * lines + line
        core = line % 2

        def part(index):
            return pl.ds(pl.multiple_of(index * CHUNK, CHUNK), CHUNK)

        rhs_in, v0_in = [], []
        for step in range(steps):
            at = pl.ds(step * CHUNK, CHUNK)
            rhs_in.append(pltpu.make_async_copy(rhs_hbm.at[at], rhs.at[at], rhs_sem.at[step]))
            v0_in.append(pltpu.make_async_copy(v_hbm.at[0, at], v.at[0, at], v0_sem.at[step]))
            rhs_in[-1].start()
            v0_in[-1].start()
        u_in = [pltpu.make_async_copy(u_hbm.at[k], u.at[k], u_sem.at[k]) for k in range(levels)]
        v_in = {k: pltpu.make_async_copy(v_hbm.at[k], v.at[k], v_sem.at[k]) for k in range(1, levels)}
        sides, cap_in = [], []
        for level in range(levels):
            child = flat // (2 ** tops[level])
            side = child % 2
            sides.append(side)
            cap_in.append(
                pltpu.make_async_copy(
                    cap_hbm.at[2**level - 1 + child // 2, pl.ds(pl.multiple_of(side * rank, rank), rank)],
                    cap.at[level],
                    cap_sem.at[level],
                )
            )
        for level in range(1, levels):
            v_in[level].start()
            u_in[level - 1].start()
        u_in[levels - 1].start()
        for copy in cap_in:
            copy.start()

        def partner(bit):
            if bit < line_bits:
                span = 2**bit
                return {"rows": line + span - 2 * span * ((line // span) % 2)}
            span = 2 ** (bit - line_bits)
            return {"leaf": leaf + span - 2 * span * ((leaf // span) % 2)}

        barrier = pltpu.get_barrier_semaphore()
        for bit in range(bits):
            pl.semaphore_signal(barrier, inc=1, device_id=partner(bit), device_id_type=MESH)
        pl.semaphore_wait(barrier, bits)

        mine = pl.ds(pl.multiple_of(core * half, half), half)
        theirs = pl.ds(pl.multiple_of((1 - core) * half, half), half)
        sent = []
        flying = [None] * levels
        stage = [0] * levels

        def send(src, dst, sem, bit):
            copy = pltpu.make_async_remote_copy(
                src_ref=src,
                dst_ref=dst,
                send_sem=tx.at[sem],
                recv_sem=rx.at[sem],
                device_id=partner(bit),
                device_id_type=MESH,
            )
            copy.start()
            sent.append(copy)
            return copy

        def begin(level):
            flying[level] = [send(acc[level].at[theirs], recv[level].at[0], first[level], 0)]

        def advance(level):
            at, top = stage[level], tops[level]
            if at > top + 1:
                return
            for copy in flying[level]:
                copy.wait_recv()
            stage[level] = at + 1
            if at < top:
                own = acc[level][mine] if at == 0 else cur[level][at - 1]
                cur[level][at] = own + recv[level][at]
                flying[level] = [
                    send(cur[level].at[at], recv[level].at[at + 1], first[level] + at + 1, at + 1)
                ]
            elif at == top:
                side = sides[level]
                base = exchanges + 2 * level
                flying[level] = [
                    send(cur[level].at[top - 1], stk[level].at[side, mine], base, 0),
                    send(recv[level].at[top], stk[level].at[1 - side, mine], base + 1, 0),
                ]
                stk[level][side, mine] = cur[level][top - 1]
                stk[level][1 - side, mine] = recv[level][top]

        for level in range(levels):
            columns = widths[level]
            if level:
                v_in[level].wait()
                u_in[level - 1].wait()

            def body(step, level=level, columns=columns):
                at = part(step)
                if level == 0:
                    high[at, :width], low[at, :width] = split(rhs[at])
                else:
                    new = slice(columns - rank, columns)
                    high[at, new], low[at, new] = split(u[level - 1, at])
                vh, vl = split(v[level, at])
                both = dot_rows(jnp.concatenate([vh, vl], axis=1), high[at, :columns])
                acc[level][...] += both[:rank] + both[rank:] + dot_rows(vh, low[at, :columns])

            acc[level][...] = jnp.zeros_like(acc[level])
            if level == 0:
                for step in range(steps):
                    rhs_in[step].wait()
                    v0_in[step].wait()
                    body(step)
            else:
                pl.loop(0, steps)(body)
            begin(level)
            for earlier in range(level):
                advance(earlier)

        u_in[levels - 1].wait()

        @pl.loop(0, steps)
        def _(step):
            at = part(step)
            new = slice(width + (levels - 1) * rank, width + levels * rank)
            high[at, new], low[at, new] = split(u[levels - 1, at])

        for copy in cap_in:
            copy.wait()
        solved = 0
        while solved < levels:
            for level in range(levels - 1, -1, -1):
                advance(level)
            while solved < levels and stage[solved] > tops[solved] + 1:
                level = solved
                proj = stk[level][:, :, :width].reshape(2 * rank, width)
                if level:
                    cross = stk[level][:, :, width:].reshape(2 * rank, level * rank)
                    proj = proj - dot3(cross, coef[: level * rank])
                coef[level * rank : (level + 1) * rank] = dot3(cap[level], proj)
                solved += 1

        out_copies = []
        ch, cl = split(coef[...])

        @pl.loop(0, steps)
        def _(step):
            at = part(step)
            uh = high[at, width:]
            ul = low[at, width:]
            rhs[at] = rhs[at] - (dot(uh, ch) + dot(uh, cl) + dot(ul, ch))
            pltpu.make_async_copy(rhs.at[at], out_hbm.at[at], out_sem.at[step]).start()

        for step in range(steps):
            at = pl.ds(step * CHUNK, CHUNK)
            pltpu.make_async_copy(rhs.at[at], out_hbm.at[at], out_sem.at[step]).wait()
        for copy in sent:
            copy.wait_send()

    scratch_shapes = [
        pltpu.VMEM((rows, width), F32),
        pltpu.VMEM((levels, rows, rank), F32),
        pltpu.VMEM((levels, rows, rank), F32),
        pltpu.VMEM((levels, rank, 2 * rank), F32),
        pltpu.VMEM((rows, width + levels * rank), BF16),
        pltpu.VMEM((rows, width + levels * rank), BF16),
        pltpu.VMEM((levels * rank, width), F32),
        *[pltpu.VMEM((rank, w), F32) for w in widths],
        *[pltpu.VMEM((top, half, w), F32) for top, w in zip(tops, widths)],
        *[pltpu.VMEM((top + 1, half, w), F32) for top, w in zip(tops, widths)],
        *[pltpu.VMEM((2, rank, w), F32) for w in widths],
        pltpu.SemaphoreType.DMA((steps,)),
        pltpu.SemaphoreType.DMA((steps,)),
        pltpu.SemaphoreType.DMA((levels,)),
        pltpu.SemaphoreType.DMA((levels,)),
        pltpu.SemaphoreType.DMA((levels,)),
        pltpu.SemaphoreType.DMA((steps,)),
        pltpu.SemaphoreType.DMA((exchanges + 2 * levels,)),
        pltpu.SemaphoreType.DMA((exchanges + 2 * levels,)),
    ]
    return kernel, scratch_shapes


def solution(mesh):
    leaves, lines = mesh.shape["leaf"], mesh.shape["rows"]

    def per_device(rhs, u_basis, v_basis, cap_inv):
        levels, rows, rank = u_basis.shape
        width = rhs.shape[1]
        kernel, scratch_shapes = make_kernel(levels, rows, rank, width, leaves, lines)
        return pl.pallas_call(
            kernel,
            out_shape=jax.ShapeDtypeStruct((rows, width), F32),
            in_specs=[pl.BlockSpec(memory_space=pl.ANY)] * 4,
            out_specs=pl.BlockSpec(memory_space=pl.ANY),
            scratch_shapes=scratch_shapes,
            compiler_params=pltpu.CompilerParams(
                collective_id=0, has_side_effects=True, vmem_limit_bytes=60 * 2**20
            ),
        )(rhs, u_basis, v_basis, cap_inv)

    in_specs = (
        P(("leaf", "rows"), None),
        P(None, ("leaf", "rows"), None),
        P(None, ("leaf", "rows"), None),
        P(),
    )
    return jax.shard_map(
        per_device, mesh=mesh, in_specs=in_specs, out_specs=P(("leaf", "rows"), None), check_vma=False
    )
```

```python
import jax
import jax.numpy as jnp
from jax import lax
from jax.experimental import pallas as pl
from jax.experimental.pallas import tpu as pltpu
from jax.sharding import PartitionSpec as P

MESH = pl.DeviceIdType.MESH
CHUNK = 512
LIMIT = 45 * 2**20
F32 = jnp.float32
BF16 = jnp.bfloat16


def split(x):
    high = x.astype(BF16)
    return high, (x - high.astype(F32)).astype(BF16)


def dot(a, b):
    return jnp.dot(a, b, preferred_element_type=F32)


def dot_rows(a, b):
    return lax.dot_general(a, b, (((0,), (0,)), ((), ())), preferred_element_type=F32)


def dot3(a, b):
    ah, al = split(a)
    bh, bl = split(b)
    return dot(ah, bh) + dot(al, bh) + dot(ah, bl)


def make_kernel(levels, rows, rank, width, leaves, lines):
    bits = (leaves * lines).bit_length() - 1
    line_bits = lines.bit_length() - 1
    half = rank // 2
    steps = rows // CHUNK
    tops = [bits - level - 1 for level in range(levels)]
    first = [sum(top + 1 for top in tops[:level]) for level in range(levels)]
    exchanges = sum(top + 1 for top in tops)
    widths = [width + level * rank for level in range(levels)]

    def kernel(rhs_hbm, u_hbm, v_hbm, cap_hbm, rhs, high, low, coef, *scratch):
        u, v, cap = scratch[:3]
        acc = scratch[3 : 3 + levels]
        cur = scratch[3 + levels : 3 + 2 * levels]
        recv = scratch[3 + 2 * levels : 3 + 3 * levels]
        stk = scratch[3 + 3 * levels : 3 + 4 * levels]
        rhs_sem, v0_sem, u_sem, v_sem, cap_sem, tx, rx = scratch[3 + 4 * levels :]

        leaf = lax.axis_index("leaf")
        line = lax.axis_index("rows")
        flat = leaf * lines + line
        core = line % 2

        def part(index):
            return pl.ds(pl.multiple_of(index * CHUNK, CHUNK), CHUNK)

        rhs_in, v0_in = [], []
        for step in range(steps):
            at = pl.ds(step * CHUNK, CHUNK)
            rhs_in.append(pltpu.make_async_copy(rhs_hbm.at[at], rhs.at[at], rhs_sem.at[step]))
            v0_in.append(pltpu.make_async_copy(v_hbm.at[0, at], v.at[0, at], v0_sem.at[step]))
            rhs_in[-1].start()
            v0_in[-1].start()
        u_in = [pltpu.make_async_copy(u_hbm.at[k], u.at[k], u_sem.at[k]) for k in range(levels)]
        v_in = {k: pltpu.make_async_copy(v_hbm.at[k], v.at[k], v_sem.at[k]) for k in range(1, levels)}
        sides, cap_in = [], []
        for level in range(levels):
            child = flat // (2 ** tops[level])
            side = child % 2
            sides.append(side)
            cap_in.append(
                pltpu.make_async_copy(
                    cap_hbm.at[2**level - 1 + child // 2, pl.ds(pl.multiple_of(side * rank, rank), rank)],
                    cap.at[level],
                    cap_sem.at[level],
                )
            )
        for level in range(1, levels):
            v_in[level].start()
            u_in[level - 1].start()
        u_in[levels - 1].start()
        for copy in cap_in:
            copy.start()

        def partner(bit):
            if bit < line_bits:
                span = 2**bit
                return {"rows": line + span - 2 * span * ((line // span) % 2)}
            span = 2 ** (bit - line_bits)
            return {"leaf": leaf + span - 2 * span * ((leaf // span) % 2)}

        barrier = pltpu.get_barrier_semaphore()
        for bit in range(bits):
            pl.semaphore_signal(barrier, inc=1, device_id=partner(bit), device_id_type=MESH)
        pl.semaphore_wait(barrier, bits)

        mine = pl.ds(pl.multiple_of(core * half, half), half)
        theirs = pl.ds(pl.multiple_of((1 - core) * half, half), half)
        sent = []
        flying = [None] * levels
        stage = [0] * levels

        def send(src, dst, sem, bit):
            copy = pltpu.make_async_remote_copy(
                src_ref=src,
                dst_ref=dst,
                send_sem=tx.at[sem],
                recv_sem=rx.at[sem],
                device_id=partner(bit),
                device_id_type=MESH,
            )
            copy.start()
            sent.append(copy)
            return copy

        def begin(level):
            flying[level] = [send(acc[level].at[theirs], recv[level].at[0], first[level], 0)]

        def advance(level):
            at, top = stage[level], tops[level]
            if at > top:
                return
            for copy in flying[level]:
                copy.wait_recv()
            stage[level] = at + 1
            if at < top:
                own = acc[level][mine] if at == 0 else cur[level][at - 1]
                cur[level][at] = own + recv[level][at]
                flying[level] = [
                    send(cur[level].at[at], recv[level].at[at + 1], first[level] + at + 1, at + 1)
                ]

        def gather(level):
            while stage[level] <= tops[level]:
                advance(level)
            top, side = tops[level], sides[level]
            pair = jnp.concatenate([cur[level][top - 1], recv[level][top]], axis=0)
            proj = pair[:, :width]
            if level:
                proj = proj - dot3(pair[:, width:], coef[: level * rank])
            stk[level][side, mine] = proj[:half]
            stk[level][1 - side, mine] = proj[half:]
            base = exchanges + 2 * level
            flying[level] = [
                send(stk[level].at[k, mine], stk[level].at[k, mine], base + k, 0) for k in range(2)
            ]

        def finish(level):
            for copy in flying[level]:
                copy.wait_recv()
            stacked = stk[level][...].reshape(2 * rank, width)
            coef[level * rank : (level + 1) * rank] = dot3(cap[level], stacked)

        for level in range(levels):
            columns = widths[level]
            if level:
                v_in[level].wait()
                u_in[level - 1].wait()

            def body(step, level=level, columns=columns):
                at = part(step)
                if level == 0:
                    high[at, :width], low[at, :width] = split(rhs[at])
                else:
                    new = slice(columns - rank, columns)
                    high[at, new], low[at, new] = split(u[level - 1, at])
                vh, vl = split(v[level, at])
                both = dot_rows(jnp.concatenate([vh, vl], axis=1), high[at, :columns])
                acc[level][...] += both[:rank] + both[rank:] + dot_rows(vh, low[at, :columns])

            acc[level][...] = jnp.zeros_like(acc[level])
            if level == 0:
                for step in range(steps):
                    rhs_in[step].wait()
                    v0_in[step].wait()
                    body(step)
            elif level < levels - 1:
                pl.loop(0, steps)(body)
            else:
                pl.loop(0, steps // 2)(body)
                for earlier in range(level):
                    advance(earlier)
                pl.loop(steps // 2, steps)(body)
            begin(level)
            for earlier in range(level):
                advance(earlier)

        advance(levels - 1)
        u_in[levels - 1].wait()

        @pl.loop(0, steps)
        def _(step):
            at = part(step)
            new = slice(width + (levels - 1) * rank, width + levels * rank)
            high[at, new], low[at, new] = split(u[levels - 1, at])

        for copy in cap_in:
            copy.wait()

        def subtract(start, stop):
            ch, cl = split(coef[: early * rank])
            used = slice(width, width + early * rank)

            @pl.loop(start, stop)
            def _(step):
                at = part(step)
                uh, ul = high[at, used], low[at, used]
                rhs[at] = rhs[at] - (dot(uh, ch) + dot(uh, cl) + dot(ul, ch))

        early = levels // 2
        for level in range(levels):
            gather(level)
            if level == early:
                subtract(0, steps // 2)
            if level == levels - 1:
                subtract(steps // 2, steps)
            finish(level)

        for copy in sent:
            copy.wait_send()

    outs = [
        pltpu.VMEM((rows, width), F32),
        pltpu.VMEM((rows, width + levels * rank), BF16),
        pltpu.VMEM((rows, width + levels * rank), BF16),
        pltpu.VMEM((levels * rank, width), F32),
    ]
    scratch_shapes = [
        pltpu.VMEM((levels, rows, rank), F32),
        pltpu.VMEM((levels, rows, rank), F32),
        pltpu.VMEM((levels, rank, 2 * rank), F32),
        *[pltpu.VMEM((rank, w), F32) for w in widths],
        *[pltpu.VMEM((top, half, w), F32) for top, w in zip(tops, widths)],
        *[pltpu.VMEM((top + 1, half, w), F32) for top, w in zip(tops, widths)],
        *[pltpu.VMEM((2, rank, width), F32) for _ in widths],
        pltpu.SemaphoreType.DMA((steps,)),
        pltpu.SemaphoreType.DMA((steps,)),
        pltpu.SemaphoreType.DMA((levels,)),
        pltpu.SemaphoreType.DMA((levels,)),
        pltpu.SemaphoreType.DMA((levels,)),
        pltpu.SemaphoreType.DMA((exchanges + 2 * levels,)),
        pltpu.SemaphoreType.DMA((exchanges + 2 * levels,)),
    ]
    return kernel, outs, scratch_shapes


def apply(rhs, high, low, coef, out_hbm, out, out_sem):
    rows, width = rhs.shape
    steps = rows // CHUNK
    early = coef.shape[0] // 2
    ch, cl = split(coef[early:])

    @pl.loop(0, steps)
    def _(step):
        at = pl.ds(pl.multiple_of(step * CHUNK, CHUNK), CHUNK)
        uh = high[at, width + early :]
        ul = low[at, width + early :]
        out[at] = rhs[at] - (dot(uh, ch) + dot(uh, cl) + dot(ul, ch))
        pltpu.make_async_copy(out.at[at], out_hbm.at[at], out_sem.at[step]).start()

    for step in range(steps):
        at = pl.ds(step * CHUNK, CHUNK)
        pltpu.make_async_copy(out.at[at], out_hbm.at[at], out_sem.at[step]).wait()


def solution(mesh):
    leaves, lines = mesh.shape["leaf"], mesh.shape["rows"]

    def per_device(rhs, u_basis, v_basis, cap_inv):
        levels, rows, rank = u_basis.shape
        width = rhs.shape[1]
        kernel, outs, scratch_shapes = make_kernel(levels, rows, rank, width, leaves, lines)
        whole = pl.BlockSpec(memory_space=pltpu.VMEM)
        kept = pl.pallas_call(
            kernel,
            out_shape=outs,
            in_specs=[pl.BlockSpec(memory_space=pl.ANY)] * 4,
            out_specs=[whole] * 4,
            scratch_shapes=scratch_shapes,
            compiler_params=pltpu.CompilerParams(
                collective_id=0, has_side_effects=True, vmem_limit_bytes=LIMIT
            ),
        )(rhs, u_basis, v_basis, cap_inv)
        return pl.pallas_call(
            apply,
            out_shape=jax.ShapeDtypeStruct((rows, width), F32),
            in_specs=[whole] * 4,
            out_specs=pl.BlockSpec(memory_space=pl.ANY),
            scratch_shapes=[pltpu.VMEM((rows, width), F32), pltpu.SemaphoreType.DMA((rows // CHUNK,))],
            compiler_params=pltpu.CompilerParams(vmem_limit_bytes=8 * 2**20),
        )(*kept)

    in_specs = (
        P(("leaf", "rows"), None),
        P(None, ("leaf", "rows"), None),
        P(None, ("leaf", "rows"), None),
        P(),
    )
    return jax.shard_map(
        per_device, mesh=mesh, in_specs=in_specs, out_specs=P(("leaf", "rows"), None), check_vma=False
    )
```

```python
import jax
import jax.numpy as jnp
from jax import lax
from jax.experimental import pallas as pl
from jax.experimental.pallas import tpu as pltpu
from jax.sharding import PartitionSpec as P

MESH = pl.DeviceIdType.MESH
CHUNK = 512
LIMIT = 45 * 2**20
PLAN = {1: ((0,), ()), 2: ((0, 1), (0, 1)), 3: ((2,), (0, 1), (2,), (1, 2))}
F32 = jnp.float32
BF16 = jnp.bfloat16


def split(x):
    high = x.astype(BF16)
    return high, (x - high.astype(F32)).astype(BF16)


def dot(a, b):
    return jnp.dot(a, b, preferred_element_type=F32)


def dot_rows(a, b):
    return lax.dot_general(a, b, (((0,), (0,)), ((), ())), preferred_element_type=F32)


def dot3(a, b):
    ah, al = split(a)
    bh, bl = split(b)
    return dot(ah, bh) + dot(al, bh) + dot(ah, bl)


def make_kernel(levels, rows, rank, width, leaves, lines):
    bits = (leaves * lines).bit_length() - 1
    line_bits = lines.bit_length() - 1
    half = rank // 2
    steps = rows // CHUNK
    tops = [bits - level - 1 for level in range(levels)]
    first = [sum(top + 1 for top in tops[:level]) for level in range(levels)]
    exchanges = sum(top + 1 for top in tops)
    widths = [width + level * rank for level in range(levels)]

    def kernel(rhs_hbm, u_hbm, v_hbm, cap_hbm, rhs, high, low, coef, *scratch):
        u, v, cap = scratch[:3]
        acc = scratch[3 : 3 + levels]
        cur = scratch[3 + levels : 3 + 2 * levels]
        recv = scratch[3 + 2 * levels : 3 + 3 * levels]
        stk = scratch[3 + 3 * levels : 3 + 4 * levels]
        rhs_sem, v0_sem, u_sem, v_sem, cap_sem, tx, rx = scratch[3 + 4 * levels :]

        leaf = lax.axis_index("leaf")
        line = lax.axis_index("rows")
        flat = leaf * lines + line
        core = line % 2

        def part(index):
            return pl.ds(pl.multiple_of(index * CHUNK, CHUNK), CHUNK)

        rhs_in, v0_in = [], []
        for step in range(steps):
            at = pl.ds(step * CHUNK, CHUNK)
            rhs_in.append(pltpu.make_async_copy(rhs_hbm.at[at], rhs.at[at], rhs_sem.at[step]))
            v0_in.append(pltpu.make_async_copy(v_hbm.at[0, at], v.at[0, at], v0_sem.at[step]))
            rhs_in[-1].start()
            v0_in[-1].start()
        u_in = [pltpu.make_async_copy(u_hbm.at[k], u.at[k], u_sem.at[k]) for k in range(levels)]
        v_in = {k: pltpu.make_async_copy(v_hbm.at[k], v.at[k], v_sem.at[k]) for k in range(1, levels)}
        sides, cap_in = [], []
        for level in range(levels):
            child = flat // (2 ** tops[level])
            side = child % 2
            sides.append(side)
            cap_in.append(
                pltpu.make_async_copy(
                    cap_hbm.at[2**level - 1 + child // 2, pl.ds(pl.multiple_of(side * rank, rank), rank)],
                    cap.at[level],
                    cap_sem.at[level],
                )
            )
        for level in range(1, levels):
            v_in[level].start()
            u_in[level - 1].start()
        u_in[levels - 1].start()
        for copy in cap_in:
            copy.start()

        def partner(bit):
            if bit < line_bits:
                span = 2**bit
                return {"rows": line + span - 2 * span * ((line // span) % 2)}
            span = 2 ** (bit - line_bits)
            return {"leaf": leaf + span - 2 * span * ((leaf // span) % 2)}

        barrier = pltpu.get_barrier_semaphore()
        for bit in range(bits):
            pl.semaphore_signal(barrier, inc=1, device_id=partner(bit), device_id_type=MESH)
        pl.semaphore_wait(barrier, bits)

        mine = pl.ds(pl.multiple_of(core * half, half), half)
        theirs = pl.ds(pl.multiple_of((1 - core) * half, half), half)
        sent = []
        flying = [None] * levels
        stage = [0] * levels

        def send(src, dst, sem, bit):
            copy = pltpu.make_async_remote_copy(
                src_ref=src,
                dst_ref=dst,
                send_sem=tx.at[sem],
                recv_sem=rx.at[sem],
                device_id=partner(bit),
                device_id_type=MESH,
            )
            copy.start()
            sent.append(copy)
            return copy

        def begin(level):
            flying[level] = [send(acc[level].at[theirs], recv[level].at[0], first[level], 0)]

        def advance(level):
            at, top = stage[level], tops[level]
            if at > top:
                return
            for copy in flying[level]:
                copy.wait_recv()
            stage[level] = at + 1
            if at < top:
                own = acc[level][mine] if at == 0 else cur[level][at - 1]
                cur[level][at] = own + recv[level][at]
                flying[level] = [
                    send(cur[level].at[at], recv[level].at[at + 1], first[level] + at + 1, at + 1)
                ]

        def gather(level):
            while stage[level] <= tops[level]:
                advance(level)
            top, side = tops[level], sides[level]
            pair = jnp.concatenate([cur[level][top - 1], recv[level][top]], axis=0)
            proj = pair[:, :width]
            if level:
                proj = proj - dot3(pair[:, width:], coef[: level * rank])
            stk[level][side, mine] = proj[:half]
            stk[level][1 - side, mine] = proj[half:]
            base = exchanges + 2 * level
            flying[level] = [
                send(stk[level].at[k, mine], stk[level].at[k, mine], base + k, 0) for k in range(2)
            ]

        def finish(level):
            for copy in flying[level]:
                copy.wait_recv()
            stacked = stk[level][...].reshape(2 * rank, width)
            coef[level * rank : (level + 1) * rank] = dot3(cap[level], stacked)

        for level in range(levels):
            columns = widths[level]
            if level:
                v_in[level].wait()
                u_in[level - 1].wait()

            def body(step, level=level, columns=columns):
                at = part(step)
                if level == 0:
                    high[at, :width], low[at, :width] = split(rhs[at])
                else:
                    new = slice(columns - rank, columns)
                    high[at, new], low[at, new] = split(u[level - 1, at])
                vh, vl = split(v[level, at])
                both = dot_rows(jnp.concatenate([vh, vl], axis=1), high[at, :columns])
                acc[level][...] += both[:rank] + both[rank:] + dot_rows(vh, low[at, :columns])

            acc[level][...] = jnp.zeros_like(acc[level])
            if level == 0:
                for step in range(steps):
                    rhs_in[step].wait()
                    v0_in[step].wait()
                    body(step)
                begin(level)
            else:
                plan = PLAN[level]
                piece = steps // len(plan)
                for k, ready in enumerate(plan):
                    pl.loop(k * piece, (k + 1) * piece)(body)
                    if k == len(plan) - 1:
                        begin(level)
                    for earlier in ready:
                        advance(earlier)

        u_in[levels - 1].wait()

        def split_last(start, stop):
            @pl.loop(start, stop)
            def _(step):
                at = part(step)
                new = slice(width + (levels - 1) * rank, width + levels * rank)
                high[at, new], low[at, new] = split(u[levels - 1, at])

        for copy in cap_in:
            copy.wait()

        def subtract(start, stop):
            ch, cl = split(coef[: early * rank])
            used = slice(width, width + early * rank)

            @pl.loop(start, stop)
            def _(step):
                at = part(step)
                uh, ul = high[at, used], low[at, used]
                rhs[at] = rhs[at] - (dot(uh, ch) + dot(uh, cl) + dot(ul, ch))

        early = levels // 2
        quarter = steps // 4
        gather(0)
        split_last(0, quarter)
        advance(levels - 1)
        split_last(quarter, 3 * quarter)
        for level in range(levels):
            if level:
                gather(level)
            if level == 1:
                split_last(3 * quarter, steps)
            if level == early:
                subtract(0, steps // 2)
            if level == levels - 1:
                subtract(steps // 2, steps)
            finish(level)

        for copy in sent:
            copy.wait_send()

    outs = [
        pltpu.VMEM((rows, width), F32),
        pltpu.VMEM((rows, width + levels * rank), BF16),
        pltpu.VMEM((rows, width + levels * rank), BF16),
        pltpu.VMEM((levels * rank, width), F32),
    ]
    scratch_shapes = [
        pltpu.VMEM((levels, rows, rank), F32),
        pltpu.VMEM((levels, rows, rank), F32),
        pltpu.VMEM((levels, rank, 2 * rank), F32),
        *[pltpu.VMEM((rank, w), F32) for w in widths],
        *[pltpu.VMEM((top, half, w), F32) for top, w in zip(tops, widths)],
        *[pltpu.VMEM((top + 1, half, w), F32) for top, w in zip(tops, widths)],
        *[pltpu.VMEM((2, rank, width), F32) for _ in widths],
        pltpu.SemaphoreType.DMA((steps,)),
        pltpu.SemaphoreType.DMA((steps,)),
        pltpu.SemaphoreType.DMA((levels,)),
        pltpu.SemaphoreType.DMA((levels,)),
        pltpu.SemaphoreType.DMA((levels,)),
        pltpu.SemaphoreType.DMA((exchanges + 2 * levels,)),
        pltpu.SemaphoreType.DMA((exchanges + 2 * levels,)),
    ]
    return kernel, outs, scratch_shapes


def apply(rhs, high, low, coef, out_hbm, out, out_sem):
    rows, width = rhs.shape
    steps = rows // CHUNK
    early = coef.shape[0] // 2
    ch, cl = split(coef[early:])

    @pl.loop(0, steps)
    def _(step):
        at = pl.ds(pl.multiple_of(step * CHUNK, CHUNK), CHUNK)
        uh = high[at, width + early :]
        ul = low[at, width + early :]
        out[at] = rhs[at] - (dot(uh, ch) + dot(uh, cl) + dot(ul, ch))
        pltpu.make_async_copy(out.at[at], out_hbm.at[at], out_sem.at[step]).start()

    for step in range(steps):
        at = pl.ds(step * CHUNK, CHUNK)
        pltpu.make_async_copy(out.at[at], out_hbm.at[at], out_sem.at[step]).wait()


def solution(mesh):
    leaves, lines = mesh.shape["leaf"], mesh.shape["rows"]

    def per_device(rhs, u_basis, v_basis, cap_inv):
        levels, rows, rank = u_basis.shape
        width = rhs.shape[1]
        kernel, outs, scratch_shapes = make_kernel(levels, rows, rank, width, leaves, lines)
        whole = pl.BlockSpec(memory_space=pltpu.VMEM)
        kept = pl.pallas_call(
            kernel,
            out_shape=outs,
            in_specs=[pl.BlockSpec(memory_space=pl.ANY)] * 4,
            out_specs=[whole] * 4,
            scratch_shapes=scratch_shapes,
            compiler_params=pltpu.CompilerParams(
                collective_id=0, has_side_effects=True, vmem_limit_bytes=LIMIT
            ),
        )(rhs, u_basis, v_basis, cap_inv)
        return pl.pallas_call(
            apply,
            out_shape=jax.ShapeDtypeStruct((rows, width), F32),
            in_specs=[whole] * 4,
            out_specs=pl.BlockSpec(memory_space=pl.ANY),
            scratch_shapes=[pltpu.VMEM((rows, width), F32), pltpu.SemaphoreType.DMA((rows // CHUNK,))],
            compiler_params=pltpu.CompilerParams(vmem_limit_bytes=8 * 2**20),
        )(*kept)

    in_specs = (
        P(("leaf", "rows"), None),
        P(None, ("leaf", "rows"), None),
        P(None, ("leaf", "rows"), None),
        P(),
    )
    return jax.shard_map(
        per_device, mesh=mesh, in_specs=in_specs, out_specs=P(("leaf", "rows"), None), check_vma=False
    )
```

```python
import jax
import jax.numpy as jnp
from jax import lax
from jax.experimental import pallas as pl
from jax.experimental.pallas import tpu as pltpu
from jax.sharding import PartitionSpec as P

MESH = pl.DeviceIdType.MESH
CHUNK = 1024
LIMIT = 45 * 2**20
PLAN = {1: ((0,), ()), 2: ((0, 1), (0, 1)), 3: ((2,), (0, 1), (2,), (1, 2))}
F32 = jnp.float32
BF16 = jnp.bfloat16


def split(x):
    high = x.astype(BF16)
    return high, (x - high.astype(F32)).astype(BF16)


def dot(a, b):
    return jnp.dot(a, b, preferred_element_type=F32)


def dot_rows(a, b):
    return lax.dot_general(a, b, (((0,), (0,)), ((), ())), preferred_element_type=F32)


def dot3(a, b):
    ah, al = split(a)
    bh, bl = split(b)
    return dot(ah, bh) + dot(al, bh) + dot(ah, bl)


def make_kernel(levels, rows, rank, width, leaves, lines):
    bits = (leaves * lines).bit_length() - 1
    line_bits = lines.bit_length() - 1
    half = rank // 2
    steps = rows // CHUNK
    tops = [bits - level - 1 for level in range(levels)]
    first = [sum(top + 1 for top in tops[:level]) for level in range(levels)]
    exchanges = sum(top + 1 for top in tops)
    widths = [width + level * rank for level in range(levels)]

    def kernel(rhs_hbm, u_hbm, v_hbm, cap_hbm, rhs, high, low, coef, *scratch):
        u, v, cap = scratch[:3]
        acc = scratch[3 : 3 + levels]
        cur = scratch[3 + levels : 3 + 2 * levels]
        recv = scratch[3 + 2 * levels : 3 + 3 * levels]
        stk = scratch[3 + 3 * levels : 3 + 4 * levels]
        rhs_sem, v0_sem, u_sem, v_sem, cap_sem, tx, rx = scratch[3 + 4 * levels :]

        leaf = lax.axis_index("leaf")
        line = lax.axis_index("rows")
        flat = leaf * lines + line
        core = line % 2

        def part(index):
            return pl.ds(pl.multiple_of(index * CHUNK, CHUNK), CHUNK)

        rhs_in, v0_in = [], []
        for step in range(steps):
            at = pl.ds(step * CHUNK, CHUNK)
            rhs_in.append(pltpu.make_async_copy(rhs_hbm.at[at], rhs.at[at], rhs_sem.at[step]))
            v0_in.append(pltpu.make_async_copy(v_hbm.at[0, at], v.at[0, at], v0_sem.at[step]))
            rhs_in[-1].start()
            v0_in[-1].start()
        u_in = [pltpu.make_async_copy(u_hbm.at[k], u.at[k], u_sem.at[k]) for k in range(levels)]
        v_in = {k: pltpu.make_async_copy(v_hbm.at[k], v.at[k], v_sem.at[k]) for k in range(1, levels)}
        sides, cap_in = [], []
        for level in range(levels):
            child = flat // (2 ** tops[level])
            side = child % 2
            sides.append(side)
            cap_in.append(
                pltpu.make_async_copy(
                    cap_hbm.at[2**level - 1 + child // 2, pl.ds(pl.multiple_of(side * rank, rank), rank)],
                    cap.at[level],
                    cap_sem.at[level],
                )
            )
        for level in range(1, levels):
            v_in[level].start()
            u_in[level - 1].start()
        u_in[levels - 1].start()
        for copy in cap_in:
            copy.start()

        def partner(bit):
            if bit < line_bits:
                span = 2**bit
                return {"rows": line + span - 2 * span * ((line // span) % 2)}
            span = 2 ** (bit - line_bits)
            return {"leaf": leaf + span - 2 * span * ((leaf // span) % 2)}

        barrier = pltpu.get_barrier_semaphore()
        for bit in range(bits):
            pl.semaphore_signal(barrier, inc=1, device_id=partner(bit), device_id_type=MESH)
        pl.semaphore_wait(barrier, bits)

        mine = pl.ds(pl.multiple_of(core * half, half), half)
        theirs = pl.ds(pl.multiple_of((1 - core) * half, half), half)
        sent = []
        flying = [None] * levels
        stage = [0] * levels

        def send(src, dst, sem, bit):
            copy = pltpu.make_async_remote_copy(
                src_ref=src,
                dst_ref=dst,
                send_sem=tx.at[sem],
                recv_sem=rx.at[sem],
                device_id=partner(bit),
                device_id_type=MESH,
            )
            copy.start()
            sent.append(copy)
            return copy

        def begin(level):
            flying[level] = [send(acc[level].at[theirs], recv[level].at[0], first[level], 0)]

        def advance(level):
            at, top = stage[level], tops[level]
            if at > top:
                return
            for copy in flying[level]:
                copy.wait_recv()
            stage[level] = at + 1
            if at < top:
                own = acc[level][mine] if at == 0 else cur[level][at - 1]
                cur[level][at] = own + recv[level][at]
                flying[level] = [
                    send(cur[level].at[at], recv[level].at[at + 1], first[level] + at + 1, at + 1)
                ]

        def gather(level):
            while stage[level] <= tops[level]:
                advance(level)
            top, side = tops[level], sides[level]
            pair = jnp.concatenate([cur[level][top - 1], recv[level][top]], axis=0)
            proj = pair[:, :width]
            if level:
                proj = proj - dot3(pair[:, width:], coef[: level * rank])
            stk[level][side, mine] = proj[:half]
            stk[level][1 - side, mine] = proj[half:]
            base = exchanges + 2 * level
            flying[level] = [
                send(stk[level].at[k, mine], stk[level].at[k, mine], base + k, 0) for k in range(2)
            ]

        def finish(level):
            for copy in flying[level]:
                copy.wait_recv()
            stacked = stk[level][...].reshape(2 * rank, width)
            coef[level * rank : (level + 1) * rank] = dot3(cap[level], stacked)

        for level in range(levels):
            columns = widths[level]
            if level:
                v_in[level].wait()
                u_in[level - 1].wait()

            def body(step, level=level, columns=columns):
                at = part(step)
                if level == 0:
                    high[at, :width], low[at, :width] = split(rhs[at])
                else:
                    new = slice(columns - rank, columns)
                    high[at, new], low[at, new] = split(u[level - 1, at])
                vh, vl = split(v[level, at])
                both = dot_rows(jnp.concatenate([vh, vl], axis=1), high[at, :columns])
                acc[level][...] += both[:rank] + both[rank:] + dot_rows(vh, low[at, :columns])

            acc[level][...] = jnp.zeros_like(acc[level])
            if level == 0:
                for step in range(steps):
                    rhs_in[step].wait()
                    v0_in[step].wait()
                    body(step)
                begin(level)
            else:
                plan = PLAN[level]
                piece = steps // len(plan)
                for k, ready in enumerate(plan):
                    pl.loop(k * piece, (k + 1) * piece)(body)
                    if k == len(plan) - 1:
                        begin(level)
                    for earlier in ready:
                        advance(earlier)

        u_in[levels - 1].wait()

        def split_last(start, stop):
            @pl.loop(start, stop)
            def _(step):
                at = part(step)
                new = slice(width + (levels - 1) * rank, width + levels * rank)
                high[at, new], low[at, new] = split(u[levels - 1, at])

        for copy in cap_in:
            copy.wait()

        def subtract(start, stop):
            ch, cl = split(coef[: early * rank])
            used = slice(width, width + early * rank)

            @pl.loop(start, stop)
            def _(step):
                at = part(step)
                uh, ul = high[at, used], low[at, used]
                rhs[at] = rhs[at] - (dot(uh, ch) + dot(uh, cl) + dot(ul, ch))

        early = levels // 2
        quarter = steps // 4
        gather(0)
        split_last(0, quarter)
        advance(levels - 1)
        split_last(quarter, 3 * quarter)
        for level in range(levels):
            if level:
                gather(level)
            if level == 1:
                split_last(3 * quarter, steps)
            if level == early:
                subtract(0, steps // 2)
            if level == levels - 1:
                subtract(steps // 2, steps)
            finish(level)

        for copy in sent:
            copy.wait_send()

    outs = [
        pltpu.VMEM((rows, width), F32),
        pltpu.VMEM((rows, width + levels * rank), BF16),
        pltpu.VMEM((rows, width + levels * rank), BF16),
        pltpu.VMEM((levels * rank, width), F32),
    ]
    scratch_shapes = [
        pltpu.VMEM((levels, rows, rank), F32),
        pltpu.VMEM((levels, rows, rank), F32),
        pltpu.VMEM((levels, rank, 2 * rank), F32),
        *[pltpu.VMEM((rank, w), F32) for w in widths],
        *[pltpu.VMEM((top, half, w), F32) for top, w in zip(tops, widths)],
        *[pltpu.VMEM((top + 1, half, w), F32) for top, w in zip(tops, widths)],
        *[pltpu.VMEM((2, rank, width), F32) for _ in widths],
        pltpu.SemaphoreType.DMA((steps,)),
        pltpu.SemaphoreType.DMA((steps,)),
        pltpu.SemaphoreType.DMA((levels,)),
        pltpu.SemaphoreType.DMA((levels,)),
        pltpu.SemaphoreType.DMA((levels,)),
        pltpu.SemaphoreType.DMA((exchanges + 2 * levels,)),
        pltpu.SemaphoreType.DMA((exchanges + 2 * levels,)),
    ]
    return kernel, outs, scratch_shapes


def apply(rhs, high, low, coef, out_hbm, out, out_sem):
    rows, width = rhs.shape
    steps = rows // CHUNK
    early = coef.shape[0] // 2
    ch, cl = split(coef[early:])

    @pl.loop(0, steps)
    def _(step):
        at = pl.ds(pl.multiple_of(step * CHUNK, CHUNK), CHUNK)
        uh = high[at, width + early :]
        ul = low[at, width + early :]
        out[at] = rhs[at] - (dot(uh, ch) + dot(uh, cl) + dot(ul, ch))
        pltpu.make_async_copy(out.at[at], out_hbm.at[at], out_sem.at[step]).start()

    for step in range(steps):
        at = pl.ds(step * CHUNK, CHUNK)
        pltpu.make_async_copy(out.at[at], out_hbm.at[at], out_sem.at[step]).wait()


def solution(mesh):
    leaves, lines = mesh.shape["leaf"], mesh.shape["rows"]

    def per_device(rhs, u_basis, v_basis, cap_inv):
        levels, rows, rank = u_basis.shape
        width = rhs.shape[1]
        kernel, outs, scratch_shapes = make_kernel(levels, rows, rank, width, leaves, lines)
        whole = pl.BlockSpec(memory_space=pltpu.VMEM)
        kept = pl.pallas_call(
            kernel,
            out_shape=outs,
            in_specs=[pl.BlockSpec(memory_space=pl.ANY)] * 4,
            out_specs=[whole] * 4,
            scratch_shapes=scratch_shapes,
            compiler_params=pltpu.CompilerParams(
                collective_id=0, has_side_effects=True, vmem_limit_bytes=LIMIT
            ),
        )(rhs, u_basis, v_basis, cap_inv)
        return pl.pallas_call(
            apply,
            out_shape=jax.ShapeDtypeStruct((rows, width), F32),
            in_specs=[whole] * 4,
            out_specs=pl.BlockSpec(memory_space=pl.ANY),
            scratch_shapes=[pltpu.VMEM((rows, width), F32), pltpu.SemaphoreType.DMA((rows // CHUNK,))],
            compiler_params=pltpu.CompilerParams(vmem_limit_bytes=8 * 2**20),
        )(*kept)

    in_specs = (
        P(("leaf", "rows"), None),
        P(None, ("leaf", "rows"), None),
        P(None, ("leaf", "rows"), None),
        P(),
    )
    return jax.shard_map(
        per_device, mesh=mesh, in_specs=in_specs, out_specs=P(("leaf", "rows"), None), check_vma=False
    )
```
